32 devices in a mesh: scene: 2 (over x), along: 16 (over z, y, core).
Axes of the slice: x: 2, y: 2, z: 4, core: 2. Of those that a mesh axis runs over, the one named last changes fastest.
Arguments:
- echoes: bfloat16 [2, 64, 16, 16, 256], P(None, ('scene', 'along')), parts along dimension 1, may hold values from -6 to 6
- integer_cell_displacement: int32 [64, 16], P(('scene', 'along')), parts along dimension 0, may hold values from 0 to 15
- fractional_level_label: int32 [64, 16], P(('scene', 'along')), parts along dimension 0, may hold values from 0 to 15
- steering: bfloat16 [2, 256, 256], replicated, may hold values from -0.25 to 0.25
- tile_anchor: int32 [32], P('scene'), parts along dimension 0, may hold values from -64 to 3904, as said below
Outputs:
- image_tiles: bfloat16 [2, 8192, 256], P(None, ('scene', 'along')), parts along dimension 1
The draws below stay inside these ranges and needn't reach their ends.
There are 2 independent parts, one for each index of `scene`. The reference program is written for one: setup_inputs(seed, part) draws one part's arguments, and reference() takes and returns one part's arrays. A program takes and returns all parts, laid end to end along the dimension named above; an argument that names none is the same for every part. Nothing has to cross between parts.
Inputs may be any that keep to these rules, and one draw needn't show every extreme that they name: tile_anchor[j] lies within 64 of j * 256.
All inputs are finite; a program needn't handle non-finite values.
Results may differ from the reference program's by a relative error of at most 0.0064.
Values may be sent and summed in bfloat16 or wider, within the bound.
A program may use at most 64 MiB of HBM per device.

```python
import math
import jax
import jax.numpy as jnp
from jax import lax

TX = 16
RX = 16
BEAMS = 256
BINS = 256
PULSE_DEV = 2
TILE_X = 256
STEPS = 16
TAPS = 8
SHIFTS = 16
FRACTION_LEVELS = 16
QUAD = 4093
WAVE_FOURTHS = 37
CHANS = 256
ECHO_TOTAL = 32
TILES = 16


def draw_tile_anchor(key, part):
    jitter = jax.random.randint(jax.random.fold_in(key, 7), (TILES,), -(TILE_X // 4), TILE_X // 4 + 1)
    return (jnp.arange(TILES, dtype=jnp.int32) * TILE_X + jitter).astype(jnp.int32)


def set_ends(array, rng, low, largest):
    longest = array.shape.index(max(array.shape))
    spots = []
    for shift in (0, 1):
        where = [jax.random.randint(jax.random.fold_in(rng, axis), (), 0, length) for axis, length in enumerate(array.shape)]
        where[longest] = (where[longest] + shift) % array.shape[longest]
        spots.append(tuple(where))
    return array.at[spots[0]].set(low).at[spots[1]].set(largest)


def block_scale(key, shape, shards, low, largest):
    def one(position, blocks):
        heights = jax.random.uniform(jax.random.fold_in(jax.random.fold_in(key, 6), position), (blocks,), jnp.float32, low / len(shards), largest / len(shards))
        return jnp.repeat(jnp.exp(heights), shape[position] // blocks).reshape((-1,) + (1,) * (len(shape) - position - 1))

    loudness = one(*shards[0])
    for cut in shards[1:]:
        loudness = loudness * one(*cut)
    return loudness


def noise(key, extent, spread, bound, split=(), kind=jnp.bfloat16):
    gain = block_scale(key, extent, split, -0.22, 0.18) if split else 1.0
    entries = jax.random.normal(key, extent, jnp.float32) * spread * gain
    return jnp.minimum(jnp.maximum(entries, -bound), bound).astype(kind)


def setup_inputs(seed: int = 0, part: int = 0) -> dict:
    seeds = jax.random.split(jax.random.key(seed), 6)
    own_keys = jax.random.split(jax.random.fold_in(seeds[5], part), 6)
    echoes = noise(own_keys[0], (2, ECHO_TOTAL, TX, RX, BINS), 1.0, 6.0, ((1, 16),))
    integer_cell_displacement = set_ends(jax.random.randint(own_keys[1], (ECHO_TOTAL, TX), 0, SHIFTS), jax.random.fold_in(own_keys[1], 1), 0, SHIFTS - 1).astype(jnp.int32)
    fractional_level_label = set_ends(jax.random.randint(own_keys[2], (ECHO_TOTAL, TX), 0, FRACTION_LEVELS), jax.random.fold_in(own_keys[2], 1), 0, FRACTION_LEVELS - 1).astype(jnp.int32)
    steering = noise(seeds[3], (2, CHANS, BEAMS), (2 * CHANS) ** -0.5, 0.25)
    tile_anchor = draw_tile_anchor(jax.random.fold_in(jax.random.fold_in(seeds[5], part), 71), part)
    return dict(echoes=echoes, integer_cell_displacement=integer_cell_displacement, fractional_level_label=fractional_level_label, steering=steering, tile_anchor=tile_anchor)


def tap_weights(integer_cell_displacement, fractional_level_label):
    fraction = fractional_level_label.astype(jnp.float32) / FRACTION_LEVELS
    tap_place = jnp.arange(TAPS, dtype=jnp.float32) - (TAPS // 2 - 1)
    displacement = tap_place[None, None, :] - fraction[..., None]
    window_taper = 0.54 + 0.46 * jnp.cos(math.pi * displacement / (TAPS // 2))
    kernel = jnp.sinc(displacement) * window_taper
    angle_turns = jnp.mod(WAVE_FOURTHS * (integer_cell_displacement * FRACTION_LEVELS + fractional_level_label), 4 * FRACTION_LEVELS).astype(jnp.float32) / (4 * FRACTION_LEVELS)
    phase_angle = 2.0 * math.pi * angle_turns
    return kernel * jnp.cos(phase_angle)[..., None], -kernel * jnp.sin(phase_angle)[..., None]


def compensate(echoes, integer_cell_displacement, fractional_level_label):
    bin_count = echoes.shape[-1]
    margin = SHIFTS // 2 + TAPS // 2
    padded = jnp.pad(echoes, ((0, 0), (0, 0), (0, 0), (0, 0), (margin, margin)))
    starts = (margin + integer_cell_displacement - SHIFTS // 2 - (TAPS // 2 - 1)).astype(jnp.int32)
    span_cells = bin_count + TAPS - 1

    def take_window(pulse_block, start):
        return lax.dynamic_slice_in_dim(pulse_block, start, span_cells, 2)

    windows = jax.vmap(jax.vmap(take_window, in_axes=(1, 0), out_axes=1), in_axes=(1, 0), out_axes=1)(padded, starts)
    coef_real, coef_imag = tap_weights(integer_cell_displacement, fractional_level_label)
    real_part = None
    imag_part = None
    for tap_index in range(TAPS):
        window_part = windows[..., tap_index:tap_index + bin_count]
        weight_real = coef_real[:, :, tap_index][:, :, None, None]
        weight_imag = coef_imag[:, :, tap_index][:, :, None, None]
        add_real = weight_real * window_part[0] - weight_imag * window_part[1]
        add_imag = weight_real * window_part[1] + weight_imag * window_part[0]
        real_part = add_real if real_part is None else real_part + add_real
        imag_part = add_imag if imag_part is None else imag_part + add_imag
    return jnp.stack([real_part, imag_part]).astype(jnp.bfloat16)


def form_beams(compensated, steering):
    pulse_count = compensated.shape[1]
    bin_count = compensated.shape[4]
    count_of_beams = steering.shape[2]
    flat_comp = compensated.reshape(2, pulse_count, -1, bin_count)
    mixer_grid = jnp.stack([jnp.concatenate([steering[0], steering[1]], 1),
                            jnp.concatenate([-steering[1], steering[0]], 1)])
    formed = jnp.einsum("pkcw,pcq->qkw", flat_comp.astype(jnp.float32), mixer_grid.astype(jnp.float32))
    return formed.reshape(2, count_of_beams, pulse_count, bin_count).astype(jnp.bfloat16)


def phase_table(count_of_beams, pulse_count, source, anchor):
    pulse_numbers = jnp.arange(pulse_count, dtype=jnp.int32)
    pixels = jnp.arange(TILE_X, dtype=jnp.int32)
    pixel_ratio = TILE_X // pulse_count
    pulse_spot = (source * pulse_count + pulse_numbers) * pixel_ratio
    offset_cells = anchor + pixels[None, :] - pulse_spot[:, None]
    beam_ids = jnp.arange(count_of_beams, dtype=jnp.int32)
    displacement_residue = jnp.mod(offset_cells, QUAD).astype(jnp.int32)
    offset_square = jnp.mod(displacement_residue * displacement_residue, QUAD).astype(jnp.int32)
    beam_square = jnp.mod(beam_ids * beam_ids, QUAD).astype(jnp.int32)
    phase_units = jnp.mod(offset_square[None] + beam_square[:, None, None] * displacement_residue[None]
                          + beam_ids[:, None, None] * offset_square[None], QUAD).astype(jnp.int32)
    phase_angle = 2.0 * math.pi * (phase_units.astype(jnp.float32) / QUAD)
    gain_norm = (STEPS * pulse_count * count_of_beams) ** -0.5
    grid_real = (gain_norm * jnp.cos(phase_angle)).astype(jnp.bfloat16)
    grid_imag = (gain_norm * jnp.sin(phase_angle)).astype(jnp.bfloat16)
    return jnp.stack([jnp.concatenate([grid_real, grid_imag], -1),
                      jnp.concatenate([-grid_imag, grid_real], -1)])


def project(beam_data, source, anchor):
    phase_grid = phase_table(beam_data.shape[1], beam_data.shape[2], source, anchor)
    summed = jnp.einsum("pakq,pakw->qw", phase_grid.astype(jnp.float32), beam_data.astype(jnp.float32))
    return summed.reshape(2, TILE_X, beam_data.shape[3])


def reference(echoes, integer_cell_displacement, fractional_level_label, steering, tile_anchor):
    beam_data = form_beams(compensate(echoes, integer_cell_displacement, fractional_level_label), steering)

    def one_tile(tile_id):
        running = jnp.zeros((2, TILE_X, BINS), jnp.float32)
        for distance in range(STEPS):
            source = tile_id - distance
            inside = source >= 0
            clamped = jnp.maximum(source, 0).astype(jnp.int32)
            pulse_block = lax.dynamic_slice_in_dim(beam_data, clamped * PULSE_DEV, PULSE_DEV, 2)
            contrib = project(pulse_block, clamped, tile_anchor[tile_id])
            running = running + jnp.where(inside, contrib, jnp.zeros_like(contrib))
        return running

    tile_sums = lax.map(one_tile, jnp.arange(TILES, dtype=jnp.int32))
    image_tiles = tile_sums.transpose(1, 0, 2, 3).reshape(2, TILES * TILE_X, BINS)
    return image_tiles.astype(jnp.bfloat16)
```

```python
import functools
import math

import jax
import jax.numpy as jnp
import numpy as np
from jax import lax
from jax.experimental import pallas as pl
from jax.experimental.pallas import tpu as pltpu
from jax.sharding import PartitionSpec as P

TILE_X = 256
STEPS = 16
TAPS = 8
SHIFTS = 16
FRACTION_LEVELS = 16
QUAD = 4093
WAVE_FOURTHS = 37
GROUP = 4
REACH = STEPS // GROUP
HALVES = 2
MESH = pl.DeviceIdType.MESH


def half_turn_fit(function, powers):
    spots = 0.5005 * np.cos(np.pi * (np.arange(400) + 0.5) / 800)
    table = np.stack([spots ** (2 * power) for power in range(powers)], 1)
    return [float(c) for c in np.linalg.lstsq(table, function(spots), rcond=None)[0]]


SIN_FIT = half_turn_fit(lambda f: np.sin(np.pi * f) / f, 5)
COS_FIT = half_turn_fit(lambda f: np.cos(np.pi * f), 6)


def horner(coefficients, square):
    value = coefficients[-1]
    for coefficient in coefficients[-2::-1]:
        value = value * square + coefficient
    return value


def tap_weights(integer_cell_displacement, fractional_level_label):
    fraction = fractional_level_label.astype(jnp.float32) / FRACTION_LEVELS
    tap_place = jnp.arange(TAPS, dtype=jnp.float32) - (TAPS // 2 - 1)
    displacement = tap_place[None, None, :] - fraction[..., None]
    window_taper = 0.54 + 0.46 * jnp.cos(math.pi * displacement / (TAPS // 2))
    kernel = jnp.sinc(displacement) * window_taper
    angle_turns = jnp.mod(
        WAVE_FOURTHS * (integer_cell_displacement * FRACTION_LEVELS + fractional_level_label),
        4 * FRACTION_LEVELS,
    ).astype(jnp.float32) / (4 * FRACTION_LEVELS)
    phase_angle = 2.0 * math.pi * angle_turns
    return (kernel * jnp.cos(phase_angle)[..., None], -kernel * jnp.sin(phase_angle)[..., None])


def beams_kernel(cells, weight_real, weight_imag, echoes, steering, beams, straight, crossed):
    _, pulses, transmitters, receivers, bins = echoes.shape
    part = bins // HALVES
    lanes = lax.broadcasted_iota(jnp.int32, (2 * receivers, bins), 1)
    reach_back = SHIFTS // 2 + TAPS // 2 - 1
    for pulse in range(pulses):

        @pl.loop(0, transmitters)
        def _(sender):
            cell = cells[pulse, sender] - reach_back
            both = jnp.concatenate([echoes[0, pulse, sender], echoes[1, pulse, sender]], 0)
            both = pltpu.roll(both.astype(jnp.float32), lax.rem(bins - cell, bins), 1)
            place = lanes + cell
            real = imag = None
            for tap in range(TAPS):
                moved = both if tap == 0 else pltpu.roll(both, bins - tap, 1)
                inside = (place >= -tap) & (place < bins - tap)
                moved = jnp.where(inside, moved, 0.0)
                a, b = moved[:receivers], moved[receivers:]
                wr = weight_real[pulse, sender * TAPS + tap]
                wi = weight_imag[pulse, sender * TAPS + tap]
                add_real = wr * a - wi * b
                add_imag = wr * b + wi * a
                real = add_real if real is None else real + add_real
                imag = add_imag if imag is None else imag + add_imag
            rows = pl.ds(pl.multiple_of(sender * receivers, receivers), receivers)
            minus = (-imag).astype(jnp.bfloat16)
            real, imag = real.astype(jnp.bfloat16), imag.astype(jnp.bfloat16)
            for half in range(HALVES):
                cut = slice(half * part, (half + 1) * part)
                straight[pulse, half, rows, :part] = real[:, cut]
                straight[pulse, half, rows, part:] = imag[:, cut]
                crossed[pulse, half, rows, :part] = minus[:, cut]
                crossed[pulse, half, rows, part:] = real[:, cut]

        contract = functools.partial(
            lax.dot_general,
            dimension_numbers=(((0,), (0,)), ((), ())),
            preferred_element_type=jnp.float32,
        )
        for half in range(HALVES):
            formed = contract(steering[0], straight[pulse, half])
            formed = formed + contract(steering[1], crossed[pulse, half])
            beams[half, pulse] = formed.astype(jnp.bfloat16)


def image_kernel(
    count, anchors, own, image, got, crossed, table, total, outgoing, incoming,
    mate_send, mate_recv, side_send, side_recv, pass_send, pass_recv, up_send, up_recv,
):
    _, pulses, beams, width = own.shape
    part = width // 2
    spacing = TILE_X // pulses
    blocks = GROUP * pulses + 1
    me = lax.axis_index("along")
    group, place = me // GROUP, me % GROUP
    groups = count // GROUP
    mate = group * GROUP + (place + 1 - 2 * (place % 2))
    side = group * GROUP + (place + 2) % GROUP
    mate_place, side_place = mate % GROUP, side % GROUP
    far_place = side_place + 1 - 2 * (side_place % 2)
    has_below, has_above = group > 0, group < groups - 1

    barrier = pltpu.get_barrier_semaphore()
    for other in (mate, side):
        pl.semaphore_signal(barrier, inc=1, device_id={"along": other}, device_id_type=MESH)

    @pl.when(has_below)
    def _():
        pl.semaphore_signal(barrier, inc=1, device_id={"along": me - GROUP}, device_id_type=MESH)

    @pl.when(has_above)
    def _():
        pl.semaphore_signal(barrier, inc=1, device_id={"along": me + GROUP}, device_id_type=MESH)

    pl.semaphore_wait(barrier, 2 + has_below.astype(jnp.int32) + has_above.astype(jnp.int32))

    def remote(source, landing, send, recv, device):
        return pltpu.make_async_remote_copy(
            src_ref=source, dst_ref=landing, send_sem=send, recv_sem=recv,
            device_id={"along": device}, device_id_type=MESH,
        )

    def to_side(half):
        return remote(own.at[half], got.at[place, half], side_send.at[half], side_recv.at[half], side)

    def to_mate(half):
        return remote(own.at[half], got.at[place, half], mate_send.at[half], mate_recv.at[half], mate)

    def pass_on(half):
        return remote(
            got.at[side_place, half], got.at[side_place, half],
            pass_send.at[half], pass_recv.at[half], mate,
        )

    def to_above(step, half):
        return remote(
            outgoing.at[step - 1, half], incoming.at[step - 1, half],
            up_send.at[step - 1, half], up_recv.at[step - 1, half], me + GROUP,
        )

    for half in range(HALVES):
        to_side(half).start()
    for half in range(HALVES):
        to_mate(half).start()

    def reaches(step):
        return group + step < groups

    gain = (STEPS * pulses * beams) ** (-0.5)
    beam = lax.broadcasted_iota(jnp.int32, (8, beams), 1)
    beam = beam.astype(jnp.float32)
    beam_square = beam * beam
    beam_square = beam_square - QUAD * jnp.floor(beam_square * (1.0 / QUAD) + 0.5)
    row = lax.broadcasted_iota(jnp.int32, (16, beams), 0)
    beam = jnp.concatenate([beam, beam], 0)
    beam_square = jnp.concatenate([beam_square, beam_square], 0)

    def wrap(value):
        return value - QUAD * jnp.floor(value * (1.0 / QUAD) + 0.5)

    for step in range(REACH, -1, -1):

        @pl.when(reaches(step))
        def _(step=step):
            tile = (group + step) * GROUP + place
            first = anchors[tile] - TILE_X * (group * GROUP + GROUP - 1) - spacing * (pulses - 1)

            @pl.loop(0, blocks * spacing // 16, unroll=4)
            def _(slab):
                offset = wrap((first + slab * 16 + row).astype(jnp.float32))
                square = wrap(offset * offset)
                units = wrap(square + beam_square * offset + beam * square)
                turn = units * (1.0 / QUAD)
                fine = turn * turn
                sine = turn * horner(SIN_FIT, fine)
                cosine = horner(COS_FIT, fine)
                rows = pl.ds(pl.multiple_of(slab * 16, 16), 16)
                table[step, rows, :beams] = (gain - (2 * gain) * (sine * sine)).astype(jnp.bfloat16)
                table[step, rows, beams:] = ((2 * gain) * sine * cosine).astype(jnp.bfloat16)

    def project(step, half):
        total[step, half] = jnp.zeros((TILE_X, width), jnp.float32)
        low = place + 1 if step == REACH else 0
        high = place + 1 if step == 0 else GROUP

        @pl.loop(low, high)
        def _(source):
            value = None
            for pulse in range(pulses):
                start = (GROUP - 1 - source) * TILE_X + spacing * (pulses - 1 - pulse)
                rows = pl.ds(pl.multiple_of(start, 128), TILE_X)
                term = jnp.dot(
                    table[step, rows, :beams], got[source, half, pulse],
                    preferred_element_type=jnp.float32,
                ) + jnp.dot(
                    table[step, rows, beams:], crossed[source, half, pulse],
                    preferred_element_type=jnp.float32,
                )
                value = term if value is None else value + term
            total[step, half] += value

    def send_up(step, half):
        outgoing[step - 1, half] = total[step, half].astype(jnp.bfloat16)
        to_above(step, half).start()

    def finish(half):
        cut = slice(half * part, (half + 1) * part)
        image[0, :, cut] = total[0, half, :, :part].astype(jnp.bfloat16)
        image[1, :, cut] = total[0, half, :, part:].astype(jnp.bfloat16)

    for half in range(HALVES):
        got[place, half] = own[half]
        to_side(half).wait_recv()
        pass_on(half).start()
        to_mate(half).wait_recv()
        pass_on(half).wait_recv()
        for source in range(GROUP):
            for pulse in range(pulses):
                crossed[source, half, pulse, :, :part] = -got[source, half, pulse, :, part:]
                crossed[source, half, pulse, :, part:] = got[source, half, pulse, :, :part]
        for step in range(REACH, -1, -1):

            @pl.when(reaches(step))
            def _(step=step, half=half):
                project(step, half)
                if step == REACH:
                    send_up(step, half)
                elif step > 0:
                    pl.when(jnp.logical_not(has_below))(lambda: send_up(step, half))

    for half in range(HALVES):
        for step in range(REACH - 1, -1, -1):

            @pl.when(has_below & reaches(step))
            def _(step=step, half=half):
                to_above(step + 1, half).wait_recv()
                total[step, half] += incoming[step, half].astype(jnp.float32)
                if step > 0:
                    send_up(step, half)

        finish(half)

    for half in range(HALVES):
        to_side(half).wait_send()
        to_mate(half).wait_send()
        pass_on(half).wait_send()
        for step in range(1, REACH + 1):
            pl.when(reaches(step))(lambda step=step, half=half: to_above(step, half).wait_send())


def local(count, echoes, integer_cell_displacement, fractional_level_label, steering, tile_anchor):
    _, pulses, transmitters, receivers, bins = echoes.shape
    channels, beams = steering.shape[1:]
    part = bins // HALVES
    width = 2 * part
    weight_real, weight_imag = tap_weights(integer_cell_displacement, fractional_level_label)
    smem = pl.BlockSpec(memory_space=pltpu.SMEM)
    vmem = pl.BlockSpec(memory_space=pltpu.VMEM)
    beam_data = pl.pallas_call(
        beams_kernel,
        out_shape=jax.ShapeDtypeStruct((HALVES, pulses, beams, width), jnp.bfloat16),
        in_specs=[smem, smem, smem, vmem, vmem],
        out_specs=vmem,
        scratch_shapes=[
            pltpu.VMEM((pulses, HALVES, channels, width), jnp.bfloat16),
            pltpu.VMEM((pulses, HALVES, channels, width), jnp.bfloat16),
        ],
        name="beams",
    )(
        integer_cell_displacement,
        weight_real.reshape(pulses, transmitters * TAPS),
        weight_imag.reshape(pulses, transmitters * TAPS),
        echoes,
        steering,
    )
    rows = (GROUP * pulses + 1) * (TILE_X // pulses)
    pair = (HALVES,)
    dma = pltpu.SemaphoreType.DMA
    return pl.pallas_call(
        functools.partial(image_kernel, count),
        out_shape=jax.ShapeDtypeStruct((2, TILE_X, bins), jnp.bfloat16),
        in_specs=[smem, vmem],
        out_specs=vmem,
        scratch_shapes=[
            pltpu.VMEM((GROUP, HALVES, pulses, beams, width), jnp.bfloat16),
            pltpu.VMEM((GROUP, HALVES, pulses, beams, width), jnp.bfloat16),
            pltpu.VMEM((REACH + 1, rows, 2 * beams), jnp.bfloat16),
            pltpu.VMEM((REACH + 1, HALVES, TILE_X, width), jnp.float32),
            pltpu.VMEM((REACH, HALVES, TILE_X, width), jnp.bfloat16),
            pltpu.VMEM((REACH, HALVES, TILE_X, width), jnp.bfloat16),
            dma(pair), dma(pair), dma(pair), dma(pair), dma(pair), dma(pair),
            dma((REACH, HALVES)), dma((REACH, HALVES)),
        ],
        compiler_params=pltpu.CompilerParams(
            collective_id=0, has_side_effects=True, vmem_limit_bytes=48 * 1024 * 1024
        ),
        name="image",
    )(tile_anchor, beam_data)


def solution(mesh):
    placed = (
        P(None, ("scene", "along"), None, None, None),
        P(("scene", "along"), None),
        P(("scene", "along"), None),
        P(),
        P("scene"),
    )
    return jax.shard_map(
        functools.partial(local, mesh.shape["along"]),
        mesh=mesh,
        in_specs=placed,
        out_specs=P(None, ("scene", "along"), None),
        check_vma=False,
    )
```

```python
import functools
import math

import jax
import jax.numpy as jnp
import numpy as np
from jax import lax
from jax.experimental import pallas as pl
from jax.experimental.pallas import tpu as pltpu
from jax.sharding import PartitionSpec as P

TILE_X = 256
STEPS = 16
TAPS = 8
SHIFTS = 16
FRACTION_LEVELS = 16
QUAD = 4093
WAVE_FOURTHS = 37
GROUP = 4
REACH = STEPS // GROUP
HALVES = 2
MESH = pl.DeviceIdType.MESH


def half_turn_fit(function, powers):
    spots = 0.5005 * np.cos(np.pi * (np.arange(400) + 0.5) / 800)
    table = np.stack([spots ** (2 * power) for power in range(powers)], 1)
    return [float(c) for c in np.linalg.lstsq(table, function(spots), rcond=None)[0]]


SIN_FIT = half_turn_fit(lambda f: np.sin(np.pi * f) / f, 5)
COS_FIT = half_turn_fit(lambda f: np.cos(np.pi * f), 6)


def horner(coefficients, square):
    value = coefficients[-1]
    for coefficient in coefficients[-2::-1]:
        value = value * square + coefficient
    return value


def wrap(value):
    return value - QUAD * jnp.floor(value * (1.0 / QUAD) + 0.5)


def tap_weights(cell, level):
    shape = (TAPS, 128)
    tap = lax.broadcasted_iota(jnp.int32, shape, 0)
    fraction = jnp.full(shape, level, jnp.int32).astype(jnp.float32) * (1.0 / FRACTION_LEVELS)
    displacement = (tap - (TAPS // 2 - 1)).astype(jnp.float32) - fraction
    short = jnp.minimum(fraction, 1.0 - fraction)
    sine = short * horner(SIN_FIT, short * short)
    sine = jnp.where(tap % 2 == (TAPS // 2) % 2, sine, -sine)
    centre = displacement == 0.0
    kernel = jnp.where(centre, 1.0, sine / (math.pi * jnp.where(centre, 1.0, displacement)))
    quarter = displacement * (1.0 / TAPS)
    quarter_sine = quarter * horner(SIN_FIT, quarter * quarter)
    kernel = kernel * (0.54 + 0.46 * (1.0 - 2.0 * (quarter_sine * quarter_sine)))
    cycle = 4 * FRACTION_LEVELS
    units = lax.rem(WAVE_FOURTHS * (cell * FRACTION_LEVELS + level), cycle)
    turn = jnp.full(shape, units, jnp.int32).astype(jnp.float32) * (1.0 / cycle)
    turn = jnp.where(turn > 0.5, turn - 1.0, turn)
    half_sine = turn * horner(SIN_FIT, turn * turn)
    half_cosine = horner(COS_FIT, turn * turn)
    real = kernel * (1.0 - 2.0 * (half_sine * half_sine))
    imag = kernel * (-2.0 * (half_sine * half_cosine))
    return real, imag


def compensate(pulse, cells, levels, echoes, straight, crossed_rows):
    _, _, transmitters, receivers, bins = echoes.shape
    part = bins // HALVES
    lanes = lax.broadcasted_iota(jnp.int32, (2 * receivers, bins), 1)
    reach_back = SHIFTS // 2 + TAPS // 2 - 1

    @pl.loop(0, transmitters, unroll=4)
    def _(sender):
        own_cell = cells[pulse, sender]
        cell = own_cell - reach_back
        weight_real, weight_imag = tap_weights(own_cell, levels[pulse, sender])
        weight_real = jnp.concatenate([weight_real] * (bins // 128), 1)
        weight_imag = jnp.concatenate([weight_imag] * (bins // 128), 1)
        both = jnp.concatenate([echoes[0, pulse, sender], echoes[1, pulse, sender]], 0)
        both = pltpu.roll(both.astype(jnp.float32), lax.rem(bins - cell, bins), 1)
        place = lanes + cell
        real = imag = None
        for tap in range(TAPS):
            moved = both if tap == 0 else pltpu.roll(both, bins - tap, 1)
            inside = (place >= -tap) & (place < bins - tap)
            moved = jnp.where(inside, moved, 0.0)
            a, b = moved[:receivers], moved[receivers:]
            wr = weight_real[tap : tap + 1]
            wi = weight_imag[tap : tap + 1]
            add_real = wr * a - wi * b
            add_imag = wr * b + wi * a
            real = add_real if real is None else real + add_real
            imag = add_imag if imag is None else imag + add_imag
        rows = pl.ds(pl.multiple_of(sender * receivers, receivers), receivers)
        minus = (-imag).astype(jnp.bfloat16)
        real, imag = real.astype(jnp.bfloat16), imag.astype(jnp.bfloat16)
        for half in range(HALVES):
            cut = slice(half * part, (half + 1) * part)
            straight[half, rows, :part] = real[:, cut]
            straight[half, rows, part:] = imag[:, cut]
            crossed_rows[half, rows, :part] = minus[:, cut]
            crossed_rows[half, rows, part:] = real[:, cut]


def image_kernel(
    count, anchors, cells, levels, echoes, steering, image,
    straight, crossed_rows, turned, got, crossed, table, total, outgoing, incoming,
    mate_send, mate_recv, side_send, side_recv, pass_send, pass_recv, up_send, up_recv,
):
    pulses = echoes.shape[1]
    beams = steering.shape[2]
    part = echoes.shape[4] // HALVES
    width = 2 * part
    spacing = TILE_X // pulses
    blocks = GROUP * pulses + 1
    me = lax.axis_index("along")
    group, place = me // GROUP, me % GROUP
    groups = count // GROUP
    mate = group * GROUP + (place + 1 - 2 * (place % 2))
    side = group * GROUP + (place + 2) % GROUP
    mate_place, side_place = mate % GROUP, side % GROUP
    far_place = side_place + 1 - 2 * (side_place % 2)
    has_below, has_above = group > 0, group < groups - 1

    barrier = pltpu.get_barrier_semaphore()
    for other in (mate, side):
        pl.semaphore_signal(barrier, inc=1, device_id={"along": other}, device_id_type=MESH)

    @pl.when(has_below)
    def _():
        pl.semaphore_signal(barrier, inc=1, device_id={"along": me - GROUP}, device_id_type=MESH)

    @pl.when(has_above)
    def _():
        pl.semaphore_signal(barrier, inc=1, device_id={"along": me + GROUP}, device_id_type=MESH)


    def remote(source, landing, send, recv, device):
        return pltpu.make_async_remote_copy(
            src_ref=source, dst_ref=landing, send_sem=send, recv_sem=recv,
            device_id={"along": device}, device_id_type=MESH,
        )

    def to_side(half, pulse):
        mine = got.at[place, half, pulse]
        return remote(mine, mine, side_send.at[half, pulse], side_recv.at[half, pulse], side)

    def to_mate(half, pulse):
        mine = got.at[place, half, pulse]
        return remote(mine, mine, mate_send.at[half, pulse], mate_recv.at[half, pulse], mate)

    def pass_on(half, pulse):
        theirs = got.at[side_place, half, pulse]
        return remote(theirs, theirs, pass_send.at[half, pulse], pass_recv.at[half, pulse], mate)

    def to_above(step, half):
        return remote(
            outgoing.at[step - 1, half], incoming.at[step - 1, half],
            up_send.at[step - 1, half], up_recv.at[step - 1, half], me + GROUP,
        )

    turned[0] = steering[0].T
    turned[1] = steering[1].T

    def form(pulse, half):
        formed = jnp.dot(turned[0], straight[half], preferred_element_type=jnp.float32)
        formed += jnp.dot(turned[1], crossed_rows[half], preferred_element_type=jnp.float32)
        got[place, half, pulse] = formed.astype(jnp.bfloat16)

    for pulse in range(pulses):
        compensate(pulse, cells, levels, echoes, straight, crossed_rows)
        form(pulse, 0)
        if pulse == 0:
            pl.semaphore_wait(
                barrier, 2 + has_below.astype(jnp.int32) + has_above.astype(jnp.int32)
            )
        to_side(0, pulse).start()
        to_mate(0, pulse).start()
        for half in range(1, HALVES):
            form(pulse, half)
    for half in range(1, HALVES):
        for pulse in range(pulses):
            to_side(half, pulse).start()
            to_mate(half, pulse).start()

    def reaches(step):
        return group + step < groups

    gain = (STEPS * pulses * beams) ** (-0.5)
    beam = lax.broadcasted_iota(jnp.int32, (8, beams), 1)
    beam = beam.astype(jnp.float32)
    beam_square = beam * beam
    beam_square = beam_square - QUAD * jnp.floor(beam_square * (1.0 / QUAD) + 0.5)
    row = lax.broadcasted_iota(jnp.int32, (16, beams), 0)
    beam = jnp.concatenate([beam, beam], 0)
    beam_square = jnp.concatenate([beam_square, beam_square], 0)

    def make_table(step):

        @pl.when(reaches(step))
        def _():
            tile = (group + step) * GROUP + place
            first = anchors[tile] - TILE_X * (group * GROUP + GROUP - 1) - spacing * (pulses - 1)

            @pl.loop(0, blocks * spacing // 16, unroll=4)
            def _(slab):
                offset = wrap((first + slab * 16 + row).astype(jnp.float32))
                square = wrap(offset * offset)
                units = wrap(square + beam_square * offset + beam * square)
                turn = units * (1.0 / QUAD)
                fine = turn * turn
                sine = turn * horner(SIN_FIT, fine)
                cosine = horner(COS_FIT, fine)
                rows = pl.ds(pl.multiple_of(slab * 16, 16), 16)
                table[step, rows, :beams] = (gain - (2 * gain) * (sine * sine)).astype(jnp.bfloat16)
                table[step, rows, beams:] = ((2 * gain) * sine * cosine).astype(jnp.bfloat16)

    for step in range(REACH, 1, -1):
        make_table(step)

    def project(step, half):
        total[step, half] = jnp.zeros((TILE_X, width), jnp.float32)
        low = place + 1 if step == REACH else 0
        high = place + 1 if step == 0 else GROUP

        @pl.loop(low, high)
        def _(source):
            value = None
            for pulse in range(pulses):
                start = (GROUP - 1 - source) * TILE_X + spacing * (pulses - 1 - pulse)
                rows = pl.ds(pl.multiple_of(start, 128), TILE_X)
                term = jnp.dot(
                    table[step, rows, :beams], got[source, half, pulse],
                    preferred_element_type=jnp.float32,
                ) + jnp.dot(
                    table[step, rows, beams:], crossed[source, half, pulse],
                    preferred_element_type=jnp.float32,
                )
                value = term if value is None else value + term
            total[step, half] += value

    def send_up(step, half):
        outgoing[step - 1, half] = total[step, half].astype(jnp.bfloat16)
        to_above(step, half).start()

    def finish(half):
        cut = slice(half * part, (half + 1) * part)
        image[0, :, cut] = total[0, half, :, :part].astype(jnp.bfloat16)
        image[1, :, cut] = total[0, half, :, part:].astype(jnp.bfloat16)

    for half in range(HALVES):
        for pulse in range(pulses):
            to_side(half, pulse).wait_recv()
            pass_on(half, pulse).start()
        for pulse in range(pulses):
            to_mate(half, pulse).wait_recv()
            pass_on(half, pulse).wait_recv()
        for source in range(GROUP):
            for pulse in range(pulses):
                crossed[source, half, pulse, :, :part] = -got[source, half, pulse, :, part:]
                crossed[source, half, pulse, :, part:] = got[source, half, pulse, :, :part]
        for step in range(REACH, -1, -1):
            if half == 0 and step <= 1:
                make_table(step)

            @pl.when(reaches(step))
            def _(step=step, half=half):
                project(step, half)
                if step == REACH:
                    send_up(step, half)
                elif step > 0:
                    pl.when(jnp.logical_not(has_below))(lambda: send_up(step, half))

    for half in range(HALVES):
        for step in range(REACH - 1, -1, -1):

            @pl.when(has_below & reaches(step))
            def _(step=step, half=half):
                to_above(step + 1, half).wait_recv()
                total[step, half] += incoming[step, half].astype(jnp.float32)
                if step > 0:
                    send_up(step, half)

        finish(half)

    for half in range(HALVES):
        for pulse in range(pulses):
            to_side(half, pulse).wait_send()
            to_mate(half, pulse).wait_send()
            pass_on(half, pulse).wait_send()
        for step in range(1, REACH + 1):
            pl.when(reaches(step))(lambda step=step, half=half: to_above(step, half).wait_send())


def local(count, echoes, integer_cell_displacement, fractional_level_label, steering, tile_anchor):
    pulses, bins = echoes.shape[1], echoes.shape[4]
    channels, beams = steering.shape[1:]
    part = bins // HALVES
    width = 2 * part
    smem = pl.BlockSpec(memory_space=pltpu.SMEM)
    vmem = pl.BlockSpec(memory_space=pltpu.VMEM)
    rows = (GROUP * pulses + 1) * (TILE_X // pulses)
    pair = (HALVES, pulses)
    dma = pltpu.SemaphoreType.DMA
    return pl.pallas_call(
        functools.partial(image_kernel, count),
        out_shape=jax.ShapeDtypeStruct((2, TILE_X, bins), jnp.bfloat16),
        in_specs=[smem, smem, smem, vmem, vmem],
        out_specs=vmem,
        scratch_shapes=[
            pltpu.VMEM((HALVES, channels, width), jnp.bfloat16),
            pltpu.VMEM((HALVES, channels, width), jnp.bfloat16),
            pltpu.VMEM((2, beams, channels), jnp.bfloat16),
            pltpu.VMEM((GROUP, HALVES, pulses, beams, width), jnp.bfloat16),
            pltpu.VMEM((GROUP, HALVES, pulses, beams, width), jnp.bfloat16),
            pltpu.VMEM((REACH + 1, rows, 2 * beams), jnp.bfloat16),
            pltpu.VMEM((REACH + 1, HALVES, TILE_X, width), jnp.float32),
            pltpu.VMEM((REACH, HALVES, TILE_X, width), jnp.bfloat16),
            pltpu.VMEM((REACH, HALVES, TILE_X, width), jnp.bfloat16),
            dma(pair), dma(pair), dma(pair), dma(pair), dma(pair), dma(pair),
            dma((REACH, HALVES)), dma((REACH, HALVES)),
        ],
        compiler_params=pltpu.CompilerParams(
            collective_id=0, has_side_effects=True, vmem_limit_bytes=48 * 1024 * 1024
        ),
        name="image",
    )(tile_anchor, integer_cell_displacement, fractional_level_label, echoes, steering)


def solution(mesh):
    placed = (
        P(None, ("scene", "along"), None, None, None),
        P(("scene", "along"), None),
        P(("scene", "along"), None),
        P(),
        P("scene"),
    )
    return jax.shard_map(
        functools.partial(local, mesh.shape["along"]),
        mesh=mesh,
        in_specs=placed,
        out_specs=P(None, ("scene", "along"), None),
        check_vma=False,
    )
```

```python
import functools
import math

import jax
import jax.numpy as jnp
import numpy as np
from jax import lax
from jax.experimental import pallas as pl
from jax.experimental.pallas import tpu as pltpu
from jax.sharding import PartitionSpec as P

TILE_X = 256
STEPS = 16
TAPS = 8
SHIFTS = 16
FRACTION_LEVELS = 16
QUAD = 4093
WAVE_FOURTHS = 37
GROUP = 4
REACH = STEPS // GROUP
HALVES = 2
MESH = pl.DeviceIdType.MESH


def half_turn_fit(function, powers):
    spots = 0.5005 * np.cos(np.pi * (np.arange(400) + 0.5) / 800)
    table = np.stack([spots ** (2 * power) for power in range(powers)], 1)
    return [float(c) for c in np.linalg.lstsq(table, function(spots), rcond=None)[0]]


SIN_FIT = half_turn_fit(lambda f: np.sin(np.pi * f) / f, 5)
COS_FIT = half_turn_fit(lambda f: np.cos(np.pi * f), 6)


def horner(coefficients, square):
    value = coefficients[-1]
    for coefficient in coefficients[-2::-1]:
        value = value * square + coefficient
    return value


def wrap(value):
    return value - QUAD * jnp.floor(value * (1.0 / QUAD) + 0.5)


def tap_weights(cell, level):
    shape = (TAPS, 128)
    tap = lax.broadcasted_iota(jnp.int32, shape, 0)
    fraction = jnp.full(shape, level, jnp.int32).astype(jnp.float32) * (1.0 / FRACTION_LEVELS)
    displacement = (tap - (TAPS // 2 - 1)).astype(jnp.float32) - fraction
    short = jnp.minimum(fraction, 1.0 - fraction)
    sine = short * horner(SIN_FIT, short * short)
    sine = jnp.where(tap % 2 == (TAPS // 2) % 2, sine, -sine)
    centre = displacement == 0.0
    kernel = jnp.where(centre, 1.0, sine / (math.pi * jnp.where(centre, 1.0, displacement)))
    quarter = displacement * (1.0 / TAPS)
    quarter_sine = quarter * horner(SIN_FIT, quarter * quarter)
    kernel = kernel * (0.54 + 0.46 * (1.0 - 2.0 * (quarter_sine * quarter_sine)))
    cycle = 4 * FRACTION_LEVELS
    units = lax.rem(WAVE_FOURTHS * (cell * FRACTION_LEVELS + level), cycle)
    turn = jnp.full(shape, units, jnp.int32).astype(jnp.float32) * (1.0 / cycle)
    turn = jnp.where(turn > 0.5, turn - 1.0, turn)
    half_sine = turn * horner(SIN_FIT, turn * turn)
    half_cosine = horner(COS_FIT, turn * turn)
    real = kernel * (1.0 - 2.0 * (half_sine * half_sine))
    imag = kernel * (-2.0 * (half_sine * half_cosine))
    return real, imag


def compensate(pulse, cells, levels, echoes, straight, crossed_rows):
    _, _, transmitters, receivers, bins = echoes.shape
    part = bins // HALVES
    lanes = lax.broadcasted_iota(jnp.int32, (2 * receivers, bins), 1)
    reach_back = SHIFTS // 2 + TAPS // 2 - 1

    @pl.loop(0, transmitters, unroll=4)
    def _(sender):
        own_cell = cells[pulse, sender]
        cell = own_cell - reach_back
        weight_real, weight_imag = tap_weights(own_cell, levels[pulse, sender])
        weight_real = jnp.concatenate([weight_real] * (bins // 128), 1)
        weight_imag = jnp.concatenate([weight_imag] * (bins // 128), 1)
        both = jnp.concatenate([echoes[0, pulse, sender], echoes[1, pulse, sender]], 0)
        both = pltpu.roll(both.astype(jnp.float32), lax.rem(bins - cell, bins), 1)
        place = lanes + cell
        real = imag = None
        for tap in range(TAPS):
            moved = both if tap == 0 else pltpu.roll(both, bins - tap, 1)
            inside = (place >= -tap) & (place < bins - tap)
            moved = jnp.where(inside, moved, 0.0)
            a, b = moved[:receivers], moved[receivers:]
            wr = weight_real[tap : tap + 1]
            wi = weight_imag[tap : tap + 1]
            add_real = wr * a - wi * b
            add_imag = wr * b + wi * a
            real = add_real if real is None else real + add_real
            imag = add_imag if imag is None else imag + add_imag
        rows = pl.ds(pl.multiple_of(sender * receivers, receivers), receivers)
        minus = (-imag).astype(jnp.bfloat16)
        real, imag = real.astype(jnp.bfloat16), imag.astype(jnp.bfloat16)
        for half in range(HALVES):
            cut = slice(half * part, (half + 1) * part)
            straight[half, rows, :part] = real[:, cut]
            straight[half, rows, part:] = imag[:, cut]
            crossed_rows[half, rows, :part] = minus[:, cut]
            crossed_rows[half, rows, part:] = real[:, cut]


def image_kernel(
    count, far_anchors, far_cells, far_levels, far_echoes, far_steering, image,
    anchors, cells, levels, echoes, steering, fetched,
    straight, crossed_rows, turned, got, crossed, table, total, outgoing, incoming,
    mate_send, mate_recv, side_send, side_recv, pass_send, pass_recv, up_send, up_recv,
):
    pulses = echoes.shape[1]
    beams = steering.shape[2]
    part = echoes.shape[4] // HALVES
    width = 2 * part
    spacing = TILE_X // pulses
    blocks = GROUP * pulses + 1
    fetches = [
        pltpu.make_async_copy(source, landing, fetched.at[number])
        for number, (source, landing) in enumerate(
            [(far_cells, cells), (far_levels, levels), (far_steering, steering), (far_anchors, anchors)]
            + [(far_echoes.at[:, pulse], echoes.at[:, pulse]) for pulse in range(pulses)]
        )
    ]
    fetch_cells, fetch_levels, fetch_steering, fetch_anchors, *fetch_echoes = fetches
    for fetch in (fetch_cells, fetch_levels, *fetch_echoes, fetch_steering, fetch_anchors):
        fetch.start()
    me = lax.axis_index("along")
    group, place = me // GROUP, me % GROUP
    groups = count // GROUP
    mate = group * GROUP + (place + 1 - 2 * (place % 2))
    side = group * GROUP + (place + 2) % GROUP
    mate_place, side_place = mate % GROUP, side % GROUP
    far_place = side_place + 1 - 2 * (side_place % 2)
    has_below, has_above = group > 0, group < groups - 1

    barrier = pltpu.get_barrier_semaphore()
    for other in (mate, side):
        pl.semaphore_signal(barrier, inc=1, device_id={"along": other}, device_id_type=MESH)

    @pl.when(has_below)
    def _():
        pl.semaphore_signal(barrier, inc=1, device_id={"along": me - GROUP}, device_id_type=MESH)

    @pl.when(has_above)
    def _():
        pl.semaphore_signal(barrier, inc=1, device_id={"along": me + GROUP}, device_id_type=MESH)


    def remote(source, landing, send, recv, device):
        return pltpu.make_async_remote_copy(
            src_ref=source, dst_ref=landing, send_sem=send, recv_sem=recv,
            device_id={"along": device}, device_id_type=MESH,
        )

    def to_side(half, pulse):
        mine = got.at[place, half, pulse]
        return remote(mine, mine, side_send.at[half, pulse], side_recv.at[half, pulse], side)

    def to_mate(half, pulse):
        mine = got.at[place, half, pulse]
        return remote(mine, mine, mate_send.at[half, pulse], mate_recv.at[half, pulse], mate)

    def pass_on(half, pulse):
        theirs = got.at[side_place, half, pulse]
        return remote(theirs, theirs, pass_send.at[half, pulse], pass_recv.at[half, pulse], mate)

    def to_above(step, half):
        return remote(
            outgoing.at[step - 1, half], incoming.at[step - 1, half],
            up_send.at[step - 1, half], up_recv.at[step - 1, half], me + GROUP,
        )

    def form(pulse, half):
        formed = jnp.dot(turned[0], straight[half], preferred_element_type=jnp.float32)
        formed += jnp.dot(turned[1], crossed_rows[half], preferred_element_type=jnp.float32)
        got[place, half, pulse] = formed.astype(jnp.bfloat16)

    for pulse in range(pulses):
        if pulse == 0:
            fetch_cells.wait()
            fetch_levels.wait()
        fetch_echoes[pulse].wait()
        compensate(pulse, cells, levels, echoes, straight, crossed_rows)
        if pulse == 0:
            fetch_steering.wait()
            turned[0] = steering[0].T
            turned[1] = steering[1].T
        form(pulse, 0)
        if pulse == 0:
            pl.semaphore_wait(
                barrier, 2 + has_below.astype(jnp.int32) + has_above.astype(jnp.int32)
            )
        to_side(0, pulse).start()
        to_mate(0, pulse).start()
        for half in range(1, HALVES):
            form(pulse, half)
    for half in range(1, HALVES):
        for pulse in range(pulses):
            to_side(half, pulse).start()
            to_mate(half, pulse).start()

    def reaches(step):
        return group + step < groups

    gain = (STEPS * pulses * beams) ** (-0.5)
    beam = lax.broadcasted_iota(jnp.int32, (8, beams), 1)
    beam = beam.astype(jnp.float32)
    beam_square = beam * beam
    beam_square = beam_square - QUAD * jnp.floor(beam_square * (1.0 / QUAD) + 0.5)
    row = lax.broadcasted_iota(jnp.int32, (16, beams), 0)
    beam = jnp.concatenate([beam, beam], 0)
    beam_square = jnp.concatenate([beam_square, beam_square], 0)

    def make_table(step):

        @pl.when(reaches(step))
        def _():
            tile = (group + step) * GROUP + place
            first = anchors[tile] - TILE_X * (group * GROUP + GROUP - 1) - spacing * (pulses - 1)

            @pl.loop(0, blocks * spacing // 16, unroll=4)
            def _(slab):
                offset = wrap((first + slab * 16 + row).astype(jnp.float32))
                square = wrap(offset * offset)
                units = wrap(square + beam_square * offset + beam * square)
                turn = units * (1.0 / QUAD)
                fine = turn * turn
                sine = turn * horner(SIN_FIT, fine)
                cosine = horner(COS_FIT, fine)
                rows = pl.ds(pl.multiple_of(slab * 16, 16), 16)
                table[step, rows, :beams] = (gain - (2 * gain) * (sine * sine)).astype(jnp.bfloat16)
                table[step, rows, beams:] = ((2 * gain) * sine * cosine).astype(jnp.bfloat16)

    fetch_anchors.wait()
    for step in range(REACH, 1, -1):
        make_table(step)

    def project(step, half):
        total[step, half] = jnp.zeros((TILE_X, width), jnp.float32)
        low = place + 1 if step == REACH else 0
        high = place + 1 if step == 0 else GROUP

        @pl.loop(low, high)
        def _(source):
            value = None
            for pulse in range(pulses):
                start = (GROUP - 1 - source) * TILE_X + spacing * (pulses - 1 - pulse)
                rows = pl.ds(pl.multiple_of(start, 128), TILE_X)
                term = jnp.dot(
                    table[step, rows, :beams], got[source, half, pulse],
                    preferred_element_type=jnp.float32,
                ) + jnp.dot(
                    table[step, rows, beams:], crossed[source, half, pulse],
                    preferred_element_type=jnp.float32,
                )
                value = term if value is None else value + term
            total[step, half] += value

    def send_up(step, half):
        outgoing[step - 1, half] = total[step, half].astype(jnp.bfloat16)
        to_above(step, half).start()

    def finish(half):
        cut = slice(half * part, (half + 1) * part)
        image[0, :, cut] = total[0, half, :, :part].astype(jnp.bfloat16)
        image[1, :, cut] = total[0, half, :, part:].astype(jnp.bfloat16)

    def collect(half):
        for pulse in range(pulses):
            to_side(half, pulse).wait_recv()
            pass_on(half, pulse).start()
        for pulse in range(pulses):
            to_mate(half, pulse).wait_recv()
            pass_on(half, pulse).wait_recv()
        for source in range(GROUP):
            for pulse in range(pulses):
                crossed[source, half, pulse, :, :part] = -got[source, half, pulse, :, part:]
                crossed[source, half, pulse, :, part:] = got[source, half, pulse, :, :part]

    def begin(step, half):

        @pl.when(reaches(step))
        def _():
            project(step, half)
            if step == REACH:
                send_up(step, half)
            elif step > 0:
                pl.when(jnp.logical_not(has_below))(lambda: send_up(step, half))

    def combine(step, half):

        @pl.when(has_below & reaches(step))
        def _():
            to_above(step + 1, half).wait_recv()
            total[step, half] += incoming[step, half].astype(jnp.float32)
            if step > 0:
                send_up(step, half)

    collect(0)
    for step in range(REACH, -1, -1):
        if step <= 1:
            make_table(step)
        begin(step, 0)
    for step in range(REACH - 1, 1, -1):
        combine(step, 0)
    collect(1)
    for step in range(REACH, 1, -1):
        begin(step, 1)
    combine(1, 0)
    for step in range(1, -1, -1):
        begin(step, 1)
    combine(0, 0)
    finish(0)
    for step in range(REACH - 1, -1, -1):
        combine(step, 1)
    finish(1)

    for half in range(HALVES):
        for pulse in range(pulses):
            to_side(half, pulse).wait_send()
            to_mate(half, pulse).wait_send()
            pass_on(half, pulse).wait_send()
        for step in range(1, REACH + 1):
            pl.when(reaches(step))(lambda step=step, half=half: to_above(step, half).wait_send())


def local(count, echoes, integer_cell_displacement, fractional_level_label, steering, tile_anchor):
    pulses, bins = echoes.shape[1], echoes.shape[4]
    channels, beams = steering.shape[1:]
    part = bins // HALVES
    width = 2 * part
    rows = (GROUP * pulses + 1) * (TILE_X // pulses)
    pair = (HALVES, pulses)
    dma = pltpu.SemaphoreType.DMA
    return pl.pallas_call(
        functools.partial(image_kernel, count),
        out_shape=jax.ShapeDtypeStruct((2, TILE_X, bins), jnp.bfloat16),
        in_specs=[pl.BlockSpec(memory_space=pltpu.HBM)] * 5,
        out_specs=pl.BlockSpec(memory_space=pltpu.VMEM),
        scratch_shapes=[
            pltpu.SMEM(tile_anchor.shape, jnp.int32),
            pltpu.SMEM(integer_cell_displacement.shape, jnp.int32),
            pltpu.SMEM(fractional_level_label.shape, jnp.int32),
            pltpu.VMEM(echoes.shape, echoes.dtype),
            pltpu.VMEM(steering.shape, steering.dtype),
            dma((4 + pulses,)),
            pltpu.VMEM((HALVES, channels, width), jnp.bfloat16),
            pltpu.VMEM((HALVES, channels, width), jnp.bfloat16),
            pltpu.VMEM((2, beams, channels), jnp.bfloat16),
            pltpu.VMEM((GROUP, HALVES, pulses, beams, width), jnp.bfloat16),
            pltpu.VMEM((GROUP, HALVES, pulses, beams, width), jnp.bfloat16),
            pltpu.VMEM((REACH + 1, rows, 2 * beams), jnp.bfloat16),
            pltpu.VMEM((REACH + 1, HALVES, TILE_X, width), jnp.float32),
            pltpu.VMEM((REACH, HALVES, TILE_X, width), jnp.bfloat16),
            pltpu.VMEM((REACH, HALVES, TILE_X, width), jnp.bfloat16),
            dma(pair), dma(pair), dma(pair), dma(pair), dma(pair), dma(pair),
            dma((REACH, HALVES)), dma((REACH, HALVES)),
        ],
        compiler_params=pltpu.CompilerParams(
            collective_id=0, has_side_effects=True, vmem_limit_bytes=67_043_328
        ),
        name="image",
    )(tile_anchor, integer_cell_displacement, fractional_level_label, echoes, steering)


def solution(mesh):
    placed = (
        P(None, ("scene", "along"), None, None, None),
        P(("scene", "along"), None),
        P(("scene", "along"), None),
        P(),
        P("scene"),
    )
    return jax.shard_map(
        functools.partial(local, mesh.shape["along"]),
        mesh=mesh,
        in_specs=placed,
        out_specs=P(None, ("scene", "along"), None),
        check_vma=False,
    )
```

```python
import functools
import math

import jax
import jax.numpy as jnp
import numpy as np
from jax import lax
from jax.experimental import pallas as pl
from jax.experimental.pallas import tpu as pltpu
from jax.sharding import PartitionSpec as P

TILE_X = 256
STEPS = 16
TAPS = 8
SHIFTS = 16
FRACTION_LEVELS = 16
QUAD = 4093
WAVE_FOURTHS = 37
GROUP = 4
REACH = STEPS // GROUP
HALVES = 2
STRIPS = 2
MESH = pl.DeviceIdType.MESH


def half_turn_fit(function, powers):
    spots = 0.5005 * np.cos(np.pi * (np.arange(400) + 0.5) / 800)
    table = np.stack([spots ** (2 * power) for power in range(powers)], 1)
    return [float(c) for c in np.linalg.lstsq(table, function(spots), rcond=None)[0]]


SIN_FIT = half_turn_fit(lambda f: np.sin(np.pi * f) / f, 5)
COS_FIT = half_turn_fit(lambda f: np.cos(np.pi * f), 6)


def horner(coefficients, square):
    value = coefficients[-1]
    for coefficient in coefficients[-2::-1]:
        value = value * square + coefficient
    return value


def wrap(value):
    return value - QUAD * jnp.floor(value * (1.0 / QUAD) + 0.5)


def tap_weights(cell, level):
    shape = (TAPS, 128)
    tap = lax.broadcasted_iota(jnp.int32, shape, 0)
    fraction = jnp.full(shape, level, jnp.int32).astype(jnp.float32) * (1.0 / FRACTION_LEVELS)
    displacement = (tap - (TAPS // 2 - 1)).astype(jnp.float32) - fraction
    short = jnp.minimum(fraction, 1.0 - fraction)
    sine = short * horner(SIN_FIT, short * short)
    sine = jnp.where(tap % 2 == (TAPS // 2) % 2, sine, -sine)
    centre = displacement == 0.0
    kernel = jnp.where(centre, 1.0, sine / (math.pi * jnp.where(centre, 1.0, displacement)))
    quarter = displacement * (1.0 / TAPS)
    quarter_sine = quarter * horner(SIN_FIT, quarter * quarter)
    kernel = kernel * (0.54 + 0.46 * (1.0 - 2.0 * (quarter_sine * quarter_sine)))
    cycle = 4 * FRACTION_LEVELS
    units = lax.rem(WAVE_FOURTHS * (cell * FRACTION_LEVELS + level), cycle)
    turn = jnp.full(shape, units, jnp.int32).astype(jnp.float32) * (1.0 / cycle)
    turn = jnp.where(turn > 0.5, turn - 1.0, turn)
    half_sine = turn * horner(SIN_FIT, turn * turn)
    half_cosine = horner(COS_FIT, turn * turn)
    real = kernel * (1.0 - 2.0 * (half_sine * half_sine))
    imag = kernel * (-2.0 * (half_sine * half_cosine))
    return real, imag


def compensate(pulse, cells, levels, echoes, straight, crossed_rows):
    _, _, transmitters, receivers, bins = echoes.shape
    part = bins // HALVES
    lanes = lax.broadcasted_iota(jnp.int32, (2 * receivers, bins), 1)
    reach_back = SHIFTS // 2 + TAPS // 2 - 1

    @pl.loop(0, transmitters, unroll=4)
    def _(sender):
        own_cell = cells[pulse, sender]
        cell = own_cell - reach_back
        weight_real, weight_imag = tap_weights(own_cell, levels[pulse, sender])
        weight_real = jnp.concatenate([weight_real] * (bins // 128), 1)
        weight_imag = jnp.concatenate([weight_imag] * (bins // 128), 1)
        both = jnp.concatenate([echoes[0, pulse, sender], echoes[1, pulse, sender]], 0)
        both = pltpu.roll(both.astype(jnp.float32), lax.rem(bins - cell, bins), 1)
        place = lanes + cell
        real = imag = None
        for tap in range(TAPS):
            moved = both if tap == 0 else pltpu.roll(both, bins - tap, 1)
            inside = (place >= -tap) & (place < bins - tap)
            moved = jnp.where(inside, moved, 0.0)
            a, b = moved[:receivers], moved[receivers:]
            wr = weight_real[tap : tap + 1]
            wi = weight_imag[tap : tap + 1]
            add_real = wr * a - wi * b
            add_imag = wr * b + wi * a
            real = add_real if real is None else real + add_real
            imag = add_imag if imag is None else imag + add_imag
        rows = pl.ds(pl.multiple_of(sender * receivers, receivers), receivers)
        minus = (-imag).astype(jnp.bfloat16)
        real, imag = real.astype(jnp.bfloat16), imag.astype(jnp.bfloat16)
        for half in range(HALVES):
            cut = slice(half * part, (half + 1) * part)
            straight[half, rows, :part] = real[:, cut]
            straight[half, rows, part:] = imag[:, cut]
            crossed_rows[half, rows, :part] = minus[:, cut]
            crossed_rows[half, rows, part:] = real[:, cut]


def image_kernel(
    count, far_anchors, far_cells, far_levels, far_echoes, far_steering, image,
    anchors, cells, levels, echoes, steering, fetched,
    straight, crossed_rows, turned, got, crossed, table, total, outgoing, incoming,
    mate_send, mate_recv, side_send, side_recv, pass_send, pass_recv, up_send, up_recv,
):
    pulses = echoes.shape[1]
    beams = steering.shape[2]
    part = echoes.shape[4] // HALVES
    width = 2 * part
    spacing = TILE_X // pulses
    blocks = GROUP * pulses + 1
    fetches = [
        pltpu.make_async_copy(source, landing, fetched.at[number])
        for number, (source, landing) in enumerate(
            [(far_cells, cells), (far_levels, levels), (far_steering, steering), (far_anchors, anchors)]
            + [(far_echoes.at[:, pulse], echoes.at[:, pulse]) for pulse in range(pulses)]
        )
    ]
    fetch_cells, fetch_levels, fetch_steering, fetch_anchors, *fetch_echoes = fetches
    for fetch in (fetch_cells, fetch_levels, *fetch_echoes, fetch_steering, fetch_anchors):
        fetch.start()
    me = lax.axis_index("along")
    group, place = me // GROUP, me % GROUP
    groups = count // GROUP
    mate = group * GROUP + (place + 1 - 2 * (place % 2))
    side = group * GROUP + (place + 2) % GROUP
    mate_place, side_place = mate % GROUP, side % GROUP
    far_place = side_place + 1 - 2 * (side_place % 2)
    has_below, has_above = group > 0, group < groups - 1

    barrier = pltpu.get_barrier_semaphore()
    for other in (mate, side):
        pl.semaphore_signal(barrier, inc=1, device_id={"along": other}, device_id_type=MESH)

    @pl.when(has_below)
    def _():
        pl.semaphore_signal(barrier, inc=1, device_id={"along": me - GROUP}, device_id_type=MESH)

    @pl.when(has_above)
    def _():
        pl.semaphore_signal(barrier, inc=1, device_id={"along": me + GROUP}, device_id_type=MESH)


    def remote(source, landing, send, recv, device):
        return pltpu.make_async_remote_copy(
            src_ref=source, dst_ref=landing, send_sem=send, recv_sem=recv,
            device_id={"along": device}, device_id_type=MESH,
        )

    def to_side(half, pulse):
        mine = got.at[place, half, pulse]
        return remote(mine, mine, side_send.at[half, pulse], side_recv.at[half, pulse], side)

    def to_mate(half, pulse):
        mine = got.at[place, half, pulse]
        return remote(mine, mine, mate_send.at[half, pulse], mate_recv.at[half, pulse], mate)

    def pass_on(half, pulse):
        theirs = got.at[side_place, half, pulse]
        return remote(theirs, theirs, pass_send.at[half, pulse], pass_recv.at[half, pulse], mate)

    strip = TILE_X // STRIPS

    def to_above(step, half, number):
        rows = pl.ds(number * strip, strip)
        return remote(
            outgoing.at[step - 1, half, rows], incoming.at[step - 1, half, rows],
            up_send.at[step - 1, half, number], up_recv.at[step - 1, half, number], me + GROUP,
        )

    def form(pulse, half):
        formed = jnp.dot(turned[0], straight[half], preferred_element_type=jnp.float32)
        formed += jnp.dot(turned[1], crossed_rows[half], preferred_element_type=jnp.float32)
        got[place, half, pulse] = formed.astype(jnp.bfloat16)

    for pulse in range(pulses):
        if pulse == 0:
            fetch_cells.wait()
            fetch_levels.wait()
        fetch_echoes[pulse].wait()
        compensate(pulse, cells, levels, echoes, straight, crossed_rows)
        if pulse == 0:
            fetch_steering.wait()
            turned[0] = steering[0].T
            turned[1] = steering[1].T
        form(pulse, 0)
        if pulse == 0:
            pl.semaphore_wait(
                barrier, 2 + has_below.astype(jnp.int32) + has_above.astype(jnp.int32)
            )
        to_side(0, pulse).start()
        to_mate(0, pulse).start()
        for half in range(1, HALVES):
            form(pulse, half)
    for half in range(1, HALVES):
        for pulse in range(pulses):
            to_side(half, pulse).start()
            to_mate(half, pulse).start()

    def reaches(step):
        return group + step < groups

    gain = (STEPS * pulses * beams) ** (-0.5)
    beam = lax.broadcasted_iota(jnp.int32, (8, beams), 1)
    beam = beam.astype(jnp.float32)
    beam_square = beam * beam
    beam_square = beam_square - QUAD * jnp.floor(beam_square * (1.0 / QUAD) + 0.5)
    row = lax.broadcasted_iota(jnp.int32, (16, beams), 0)
    beam = jnp.concatenate([beam, beam], 0)
    beam_square = jnp.concatenate([beam_square, beam_square], 0)

    def make_table(step):

        @pl.when(reaches(step))
        def _():
            tile = (group + step) * GROUP + place
            first = anchors[tile] - TILE_X * (group * GROUP + GROUP - 1) - spacing * (pulses - 1)

            @pl.loop(0, blocks * spacing // 16, unroll=4)
            def _(slab):
                offset = wrap((first + slab * 16 + row).astype(jnp.float32))
                square = wrap(offset * offset)
                units = wrap(square + beam_square * offset + beam * square)
                turn = units * (1.0 / QUAD)
                fine = turn * turn
                sine = turn * horner(SIN_FIT, fine)
                cosine = horner(COS_FIT, fine)
                rows = pl.ds(pl.multiple_of(slab * 16, 16), 16)
                table[step, rows, :beams] = (gain - (2 * gain) * (sine * sine)).astype(jnp.bfloat16)
                table[step, rows, beams:] = ((2 * gain) * sine * cosine).astype(jnp.bfloat16)

    fetch_anchors.wait()

    def project(step, half):
        total[step, half] = jnp.zeros((TILE_X, width), jnp.float32)
        low = place + 1 if step == REACH else 0
        high = place + 1 if step == 0 else GROUP

        @pl.loop(low, high)
        def _(source):
            value = None
            for pulse in range(pulses):
                start = (GROUP - 1 - source) * TILE_X + spacing * (pulses - 1 - pulse)
                rows = pl.ds(pl.multiple_of(start, 128), TILE_X)
                term = jnp.dot(
                    table[step, rows, :beams], got[source, half, pulse],
                    preferred_element_type=jnp.float32,
                ) + jnp.dot(
                    table[step, rows, beams:], crossed[source, half, pulse],
                    preferred_element_type=jnp.float32,
                )
                value = term if value is None else value + term
            total[step, half] += value

    def send_strip(step, half, number):
        rows = pl.ds(number * strip, strip)
        outgoing[step - 1, half, rows] = total[step, half, rows].astype(jnp.bfloat16)
        to_above(step, half, number).start()

    def send_up(step, half):
        for number in range(STRIPS):
            send_strip(step, half, number)

    def finish(half):
        cut = slice(half * part, (half + 1) * part)
        image[0, :, cut] = total[0, half, :, :part].astype(jnp.bfloat16)
        image[1, :, cut] = total[0, half, :, part:].astype(jnp.bfloat16)

    def forward(half, pulse):
        to_side(half, pulse).wait_recv()
        pass_on(half, pulse).start()

    def collect(half):
        for pulse in range(pulses):
            to_mate(half, pulse).wait_recv()
            pass_on(half, pulse).wait_recv()
        for source in range(GROUP):
            for pulse in range(pulses):
                crossed[source, half, pulse, :, :part] = -got[source, half, pulse, :, part:]
                crossed[source, half, pulse, :, part:] = got[source, half, pulse, :, :part]

    def begin(step, half):

        @pl.when(reaches(step))
        def _():
            project(step, half)
            if step == REACH:
                send_up(step, half)
            elif step > 0:
                pl.when(jnp.logical_not(has_below))(lambda: send_up(step, half))

    def combine(step, half):

        @pl.when(has_below & reaches(step))
        def _():
            for number in range(STRIPS):
                rows = pl.ds(number * strip, strip)
                to_above(step + 1, half, number).wait_recv()
                total[step, half, rows] += incoming[step, half, rows].astype(jnp.float32)
                if step > 0:
                    send_strip(step, half, number)

    for step in range(REACH, 2, -1):
        make_table(step)
    forward(0, 0)
    make_table(2)
    for pulse in range(1, pulses):
        forward(0, pulse)
    for half in range(HALVES):
        if half > 0:
            for pulse in range(pulses):
                forward(half, pulse)
        collect(half)
        for step in range(REACH, 1, -1):
            begin(step, half)
        if half > 0:
            combine(1, half - 1)
        for step in range(1, -1, -1):
            if half == 0:
                make_table(step)
            begin(step, half)
        for step in range(REACH - 1, 1, -1):
            combine(step, half)
    combine(1, HALVES - 1)
    for half in range(HALVES):
        combine(0, half)
        finish(half)

    for half in range(HALVES):
        for pulse in range(pulses):
            to_side(half, pulse).wait_send()
            to_mate(half, pulse).wait_send()
            pass_on(half, pulse).wait_send()
        for step in range(1, REACH + 1):
            for number in range(STRIPS):
                pl.when(reaches(step))(to_above(step, half, number).wait_send)


def local(count, echoes, integer_cell_displacement, fractional_level_label, steering, tile_anchor):
    pulses, bins = echoes.shape[1], echoes.shape[4]
    channels, beams = steering.shape[1:]
    part = bins // HALVES
    width = 2 * part
    rows = (GROUP * pulses + 1) * (TILE_X // pulses)
    pair = (HALVES, pulses)
    dma = pltpu.SemaphoreType.DMA
    return pl.pallas_call(
        functools.partial(image_kernel, count),
        out_shape=jax.ShapeDtypeStruct((2, TILE_X, bins), jnp.bfloat16),
        in_specs=[pl.BlockSpec(memory_space=pltpu.HBM)] * 5,
        out_specs=pl.BlockSpec(memory_space=pltpu.VMEM),
        scratch_shapes=[
            pltpu.SMEM(tile_anchor.shape, jnp.int32),
            pltpu.SMEM(integer_cell_displacement.shape, jnp.int32),
            pltpu.SMEM(fractional_level_label.shape, jnp.int32),
            pltpu.VMEM(echoes.shape, echoes.dtype),
            pltpu.VMEM(steering.shape, steering.dtype),
            dma((4 + pulses,)),
            pltpu.VMEM((HALVES, channels, width), jnp.bfloat16),
            pltpu.VMEM((HALVES, channels, width), jnp.bfloat16),
            pltpu.VMEM((2, beams, channels), jnp.bfloat16),
            pltpu.VMEM((GROUP, HALVES, pulses, beams, width), jnp.bfloat16),
            pltpu.VMEM((GROUP, HALVES, pulses, beams, width), jnp.bfloat16),
            pltpu.VMEM((REACH + 1, rows, 2 * beams), jnp.bfloat16),
            pltpu.VMEM((REACH + 1, HALVES, TILE_X, width), jnp.float32),
            pltpu.VMEM((REACH, HALVES, TILE_X, width), jnp.bfloat16),
            pltpu.VMEM((REACH, HALVES, TILE_X, width), jnp.bfloat16),
            dma(pair), dma(pair), dma(pair), dma(pair), dma(pair), dma(pair),
            dma((REACH, HALVES, STRIPS)), dma((REACH, HALVES, STRIPS)),
        ],
        compiler_params=pltpu.CompilerParams(
            collective_id=0, has_side_effects=True, vmem_limit_bytes=67_043_328
        ),
        name="image",
    )(tile_anchor, integer_cell_displacement, fractional_level_label, echoes, steering)


def solution(mesh):
    placed = (
        P(None, ("scene", "along"), None, None, None),
        P(("scene", "along"), None),
        P(("scene", "along"), None),
        P(),
        P("scene"),
    )
    return jax.shard_map(
        functools.partial(local, mesh.shape["along"]),
        mesh=mesh,
        in_specs=placed,
        out_specs=P(None, ("scene", "along"), None),
        check_vma=False,
    )
```
